32 devices in a mesh: grp: 2 (over y), ek: 8 (over z, x), per: 2 (over core).
Axes of the slice: x: 2, y: 2, z: 4, core: 2. Of those that a mesh axis runs over, the one named last changes fastest.
Arguments:
- retarded: bfloat16 [2, 32, 2, 640, 640], P('per', ('grp', 'ek')), parts along dimension 1, may hold values from -0.25 to 0.25
- scatter_root: float32 [2, 32, 640], P('per', ('grp', 'ek')), parts along dimension 1, may hold values from 0.2 to 1
- coupling: bfloat16 [640, 640], replicated, may hold values from -0.15625 to 0.15625
- source_index: int32 [16, 16], replicated, may hold values from 0 to 15
- kernel_weight: float32 [16, 16], replicated, may hold values from 0.02 to 0.5
Outputs:
- sigma_less: bfloat16 [2, 32, 2, 640, 640], P('per', 'grp', None, 'ek'), parts along dimension 1
The draws below stay inside these ranges and needn't reach their ends.
There are 2 independent parts, one for each index of `grp`. The reference program is written for one: setup_inputs(seed, part) draws one part's arguments, and reference() takes and returns one part's arrays. A program takes and returns all parts, laid end to end along the dimension named above; an argument that names none is the same for every part. Nothing has to cross between parts.
Inputs may be any that keep to these rules, and one draw needn't show every extreme that they name: `source_index`: source energy-k points of the phonon and roughness kernel.
All inputs are finite; a program needn't handle non-finite values.
Results may differ from the reference program's by a relative error of at most 0.0055.
Values may be sent and summed in bfloat16 or wider, within the bound.
A program may use at most 64 MiB of HBM per device.

```python
import math
import jax
import jax.numpy as jnp
from jax import lax

NS = 640
TAPS = 16
POINTS = 16
PERIODS = 2


def touch_ends(entries, rng, low, largest):
    index_at = [jax.random.randint(jax.random.fold_in(rng, axis), (), 0, length) for axis, length in enumerate(entries.shape)]
    longest = entries.shape.index(max(entries.shape))
    beside = index_at[:longest] + [(index_at[longest] + 1) % entries.shape[longest]] + index_at[longest + 1:]
    return entries.at[tuple(index_at)].set(low).at[tuple(beside)].set(largest)


def steps_of(stream_key, shape, shards, least, high):
    def one(axis_at, blocks):
        draws = jax.random.uniform(jax.random.fold_in(jax.random.fold_in(stream_key, 6), axis_at), (blocks,), jnp.float32, least / len(shards), high / len(shards))
        return jnp.repeat(jnp.exp(draws), shape[axis_at] // blocks).reshape((-1,) + (1,) * (len(shape) - axis_at - 1))

    loudness = one(*shards[0])
    for cut in shards[1:]:
        loudness = loudness * one(*cut)
    return loudness


def centred(rng, dims, deviation, limit, cuts=(), held_as=jnp.bfloat16):
    result = jax.random.normal(rng, dims, jnp.float32) * deviation
    if len(cuts) > 0:
        result = steps_of(rng, dims, cuts, -0.22, 0.18) * result
    return jnp.clip(result, min=-limit, max=limit).astype(held_as)


def setup_inputs(seed: int = 0, part: int = 0) -> dict:
    keys = jax.random.split(jax.random.key(seed), 6)
    part_keys = jax.random.split(jax.random.fold_in(keys[5], part), 6)
    retarded = centred(part_keys[0], (PERIODS, POINTS, 2, NS, NS), NS ** -0.5, 0.25, ((0, 2), (1, 8)))
    scatter_root = jnp.clip(jnp.exp(math.log(1.0) - 1.609438 * jax.random.uniform(part_keys[1], (PERIODS, POINTS, NS), jnp.float32) ** steps_of(part_keys[1], (PERIODS, POINTS, NS), ((0, 2), (1, 8)), -0.2, 0.2)), 0.2, 1.0)
    coupling = centred(keys[2], (NS, NS), (2 * NS) ** -0.5, 0.15625)
    source_index = touch_ends(jax.random.randint(keys[3], (POINTS, TAPS), 0, POINTS), jax.random.fold_in(keys[3], 1), 0, POINTS - 1).astype(jnp.int32)
    kernel_weight = jnp.clip(jnp.exp(jax.random.uniform(keys[4], (POINTS, TAPS), jnp.float32, math.log(0.02), math.log(0.5))), 0.02, 0.5)
    return {"retarded": retarded, "scatter_root": scatter_root, "coupling": coupling, "source_index": source_index, "kernel_weight": kernel_weight}


def product(former, latter):
    return jnp.dot(former, latter, preferred_element_type=jnp.float32)


def transposed_product(former, latter):
    return lax.dot_general(former, latter, (((1,), (1,)), ((), ())), preferred_element_type=jnp.float32)


def build_kernel(source_index, kernel_weight, total_points):
    targets = jnp.arange(total_points, dtype=jnp.int32)
    matches = (source_index[:, :, None] == targets[None, None, :]).astype(jnp.float32)
    return jnp.sum(kernel_weight[:, :, None] * matches, axis=1).astype(jnp.bfloat16)


def local_parts(real_g, imag_g, amplitude):
    root_real = (real_g * amplitude[None, :]).astype(jnp.bfloat16)
    root_imag = (imag_g * amplitude[None, :]).astype(jnp.bfloat16)
    local_real = transposed_product(root_real, root_real) + transposed_product(root_imag, root_imag)
    skewed = transposed_product(root_imag, root_real)
    return local_real, skewed - skewed.T


def coupled_parts(real_g, imag_g, coupling):
    return product(real_g, coupling).astype(jnp.bfloat16), product(imag_g, coupling).astype(jnp.bfloat16)


def advance(local_real, local_imag, coupled_real, coupled_imag, prev_real, prev_imag):
    carried_real = (product(coupled_real, prev_real) - product(coupled_imag, prev_imag)).astype(jnp.bfloat16)
    carried_imag = (product(coupled_real, prev_imag) + product(coupled_imag, prev_real)).astype(jnp.bfloat16)
    new_real = local_real + transposed_product(carried_real, coupled_real) + transposed_product(carried_imag, coupled_imag)
    new_imag = local_imag + transposed_product(carried_imag, coupled_real) - transposed_product(carried_real, coupled_imag)
    return jnp.stack([new_real.astype(jnp.bfloat16), new_imag.astype(jnp.bfloat16)])


def reference(retarded, scatter_root, coupling, source_index, kernel_weight):
    kernel = build_kernel(source_index, kernel_weight, POINTS)
    previous = jnp.zeros((POINTS, 2, NS, NS), jnp.bfloat16)
    outputs = []
    for period in range(PERIODS):
        def one_point(operands):
            green_pair, amplitude, before = operands
            local_real, local_imag = local_parts(green_pair[0], green_pair[1], amplitude)
            coupled_real, coupled_imag = coupled_parts(green_pair[0], green_pair[1], coupling)
            return advance(local_real, local_imag, coupled_real, coupled_imag, before[0], before[1])

        previous = lax.map(one_point, (retarded[period], scatter_root[period], previous))
        convolved = product(kernel, previous.reshape(POINTS, -1)).astype(jnp.bfloat16)
        outputs.append(convolved.reshape(POINTS, 2, NS, NS))
    return jnp.stack(outputs)
```

```python
import jax
import jax.numpy as jnp
from jax import lax
from jax.experimental import pallas as pl
from jax.experimental.pallas import tpu as pltpu
from jax.sharding import PartitionSpec as P


def shifted(array, axis, by):
    size = lax.axis_size(axis)
    pairs = [(i, i + by) for i in range(size) if 0 <= i + by < size]
    return lax.ppermute(array, axis, pairs)


def product(former, latter):
    return jnp.dot(former, latter, preferred_element_type=jnp.float32)


def transposed_product(former, latter):
    return lax.dot_general(
        former, latter, (((1,), (1,)), ((), ())), preferred_element_type=jnp.float32
    )


def build_kernel(source_index, kernel_weight, total_points):
    targets = jnp.arange(total_points, dtype=jnp.int32)
    matches = (source_index[:, :, None] == targets[None, None, :]).astype(jnp.float32)
    return jnp.sum(kernel_weight[:, :, None] * matches, axis=1).astype(jnp.bfloat16)


def local_parts(real_g, imag_g, amplitude):
    root_real = (real_g * amplitude[None, :]).astype(jnp.bfloat16)
    root_imag = (imag_g * amplitude[None, :]).astype(jnp.bfloat16)
    local_real = transposed_product(root_real, root_real) + transposed_product(root_imag, root_imag)
    skewed = transposed_product(root_imag, root_real)
    return (local_real, skewed - skewed.T)


def coupled_parts(real_g, imag_g, coupling):
    return (
        product(real_g, coupling).astype(jnp.bfloat16),
        product(imag_g, coupling).astype(jnp.bfloat16),
    )


def advance(local_pair, coupled_pair, carried_in):
    coupled_real, coupled_imag = coupled_pair
    prev_real = carried_in[0]
    prev_imag = carried_in[1]
    carried_real = (product(coupled_real, prev_real) - product(coupled_imag, prev_imag)).astype(
        jnp.bfloat16
    )
    carried_imag = (product(coupled_real, prev_imag) + product(coupled_imag, prev_real)).astype(
        jnp.bfloat16
    )
    new_real = (
        local_pair[0]
        + transposed_product(carried_real, coupled_real)
        + transposed_product(carried_imag, coupled_imag)
    )
    new_imag = (
        local_pair[1]
        + transposed_product(carried_imag, coupled_real)
        - transposed_product(carried_real, coupled_imag)
    )
    return jnp.stack([new_real.astype(jnp.bfloat16), new_imag.astype(jnp.bfloat16)])


def body(retarded, scatter_root, coupling, source_index, kernel_weight):
    points_dev = retarded.shape[1]
    states = retarded.shape[3]
    groups = lax.axis_size("ek")
    total_points = points_dev * groups
    row_count = states // groups
    kernel = build_kernel(source_index, kernel_weight, total_points)
    local_terms = []
    coupled_terms = []
    lesser = []
    for member in range(points_dev):
        real_g = retarded[0, member, 0]
        imag_g = retarded[0, member, 1]
        local_pair = local_parts(real_g, imag_g, scatter_root[0, member])
        local_terms.append(local_pair)
        coupled_terms.append(coupled_parts(real_g, imag_g, coupling))
        lesser.append(
            jnp.stack([local_pair[0].astype(jnp.bfloat16), local_pair[1].astype(jnp.bfloat16)])
        )
    carried = shifted(jnp.stack(lesser), "per", 1)
    lesser = [
        advance(local_terms[member], coupled_terms[member], carried[member])
        for member in range(points_dev)
    ]
    stacked = jnp.stack(lesser)[None]
    regrouped = lax.all_to_all(stacked, "ek", split_axis=3, concat_axis=1, tiled=True)
    summed = product(kernel, regrouped.reshape(total_points, -1))
    return summed.astype(jnp.bfloat16).reshape(1, total_points, 2, row_count, states)


SUB = 16
LIMIT = 58
MESH = pl.DeviceIdType.MESH


def fused(
    retarded,
    scatter_ref,
    coupling_ref,
    index_ref,
    weight_ref,
    out,
    green,
    scatter,
    coupling,
    index,
    weight,
    stack,
    pair,
    moved,
    total,
    blocks,
    before,
    cross,
    diag,
    got_x,
    got_c,
    got_d,
    got_o,
    res_c,
    res_d,
    inner,
    result,
    spread,
    spread_d,
    load_sem,
    small_sem,
    keep_x,
    keep_c,
    keep_d,
    x_send,
    x_recv,
    c_send,
    c_side,
    c_on,
    c_recv,
    d_send,
    d_side,
    d_recv,
    o_send,
    o_on,
    o_recv,
    hand_sem,
    take_sem,
    out_sem,
):
    groups, points = got_x.shape[:2]
    me = lax.axis_index("ek")
    period = lax.axis_index("per")
    states = green.shape[2]
    wide = states // 2
    level = states // 4
    rows = states // groups
    count = points * groups

    half = me // 4
    place = me // 2
    side = me % 2
    low = place % 2
    far = 1 - half
    entry = 1 + half
    other = 4 * half + 1 - place
    beside = 2 * place + 1 - side
    across = 2 * other + side
    far_near = 2 * (2 - half) + side
    far_end = 2 * (3 * far) + side
    at_entry = place == entry

    def load(point, part):
        return pltpu.make_async_copy(
            retarded.at[0, point, part], green.at[point, part], load_sem.at[point, part]
        )

    small = [
        pltpu.make_async_copy(scatter_ref, scatter, small_sem.at[0]),
        pltpu.make_async_copy(coupling_ref, coupling, small_sem.at[1]),
        pltpu.make_async_copy(index_ref, index, small_sem.at[2]),
        pltpu.make_async_copy(weight_ref, weight, small_sem.at[3]),
    ]
    small[0].start()
    for part in range(2):
        load(0, part).start()
    small[1].start()
    for part in range(2):
        load(1, part).start()
    small[2].start()
    small[3].start()

    barrier = pltpu.get_barrier_semaphore()
    for step in range(1, groups):
        pl.semaphore_signal(
            barrier, inc=1, device_id={"ek": (me + step) % groups}, device_id_type=MESH
        )
    pl.semaphore_signal(barrier, inc=1, device_id={"per": 1 - period}, device_id_type=MESH)

    def span(start, size):
        return pl.ds(pl.multiple_of(start, SUB), size)

    def remote(source, target, sent, landed, device):
        return pltpu.make_async_remote_copy(
            src_ref=source,
            dst_ref=target,
            send_sem=sent,
            recv_sem=landed,
            device_id={"ek": device},
            device_id_type=MESH,
        )

    def send_x(point, device):
        return remote(
            blocks.at[point, 1 - device // 4, span(device * rows, rows), :],
            got_x.at[me, point],
            x_send.at[device, point],
            x_recv.at[me, point],
            device,
        )

    def wait_x(point, device):
        remote(
            got_x.at[device, point],
            got_x.at[device, point],
            x_send.at[device, point],
            x_recv.at[device, point],
            device,
        ).wait_recv()

    def send_c(point, which, slot, device):
        return remote(
            cross.at[which, point],
            got_c.at[me, point],
            c_send.at[slot, point],
            c_recv.at[me, point],
            device,
        )

    def side_c(point, source):
        here = got_c.at[source, point]
        return remote(here, here, c_side.at[source, point], c_recv.at[source, point], beside)

    def on_c(point, source, slot):
        here = got_c.at[source, point]
        return remote(here, here, c_on.at[slot, point], c_recv.at[source, point], across)

    def send_d(which, bit, slot, device):
        return remote(
            diag.at[which, bit], got_d.at[me], d_send.at[slot], d_recv.at[me], device
        )

    def side_d(source):
        here = got_d.at[source]
        return remote(here, here, d_side.at[source], d_recv.at[source], beside)

    def send_o():
        slot = jnp.where(at_entry, 0, 1)
        return remote(
            diag.at[far, far], got_o.at[slot], o_send, o_recv.at[slot], far_near
        )

    def wait_o(slot, source):
        remote(
            got_o.at[slot], got_o.at[slot], o_on.at[slot], o_recv.at[slot], source
        ).wait_recv()

    def on_o(slot, source):
        return remote(
            got_o.at[slot], got_d.at[source], o_on.at[slot], d_recv.at[source], across
        )

    def hand(point):
        return pltpu.make_async_remote_copy(
            src_ref=blocks.at[point],
            dst_ref=before.at[point],
            send_sem=hand_sem.at[point],
            recv_sem=take_sem.at[point],
            device_id={"per": 1 - period},
            device_id_type=MESH,
        )

    def own_x(point):
        return pltpu.make_async_copy(
            blocks.at[point, far, span(me * rows, rows), :], got_x.at[me, point], keep_x.at[point]
        )

    def own_c(point):
        return pltpu.make_async_copy(
            cross.at[half, point], got_c.at[me, point], keep_c.at[point]
        )

    def own_d():
        return pltpu.make_async_copy(diag.at[half, low], got_d.at[me], keep_d)

    def fill_stack(point):
        for part in range(2):
            load(point, part).wait()
        scale = scatter[0, pl.ds(point, 1), :]
        for band in range(2):
            at = slice(band * wide, (band + 1) * wide)
            real = (green[point, 0, at, :].astype(jnp.float32) * scale).astype(jnp.bfloat16)
            imag = (green[point, 1, at, :].astype(jnp.float32) * scale).astype(jnp.bfloat16)
            top = slice(band * states, band * states + wide)
            low_at = slice(band * states + wide, (band + 1) * states)
            stack[top, :states] = real
            stack[top, states:] = imag
            stack[low_at, :states] = -imag
            stack[low_at, states:] = real

    def fill_pair(point):
        @pl.loop(0, 2)
        def _(band):
            at = span(band * wide, wide)
            real = product(green[point, 0, at, :], coupling[...]).astype(jnp.bfloat16)
            imag = product(green[point, 1, at, :], coupling[...]).astype(jnp.bfloat16)
            top = span(band * states, wide)
            low_at = span(band * states + wide, wide)
            pair[top, :states] = real
            pair[top, states:] = imag
            pair[low_at, :states] = -imag
            pair[low_at, states:] = real

    def fill_moved(point):
        @pl.loop(0, 2)
        def _(band):
            at = span(band * wide, wide)
            top = span(band * states, wide)
            for part in range(2):
                straight = product(pair[top, :states], before[point, part])
                turned = product(pair[top, states:], before[point, part])
                real = straight[:, :wide] - turned[:, wide:]
                imag = straight[:, wide:] + turned[:, :wide]
                moved[at, part * wide : (part + 1) * wide] = real.astype(jnp.bfloat16)
                moved[at, states + part * wide : states + (part + 1) * wide] = imag.astype(
                    jnp.bfloat16
                )

    def block(upper, lower):
        total[...] = transposed_product(
            stack[span(upper * states, wide), :], stack[span(lower * states, states), :]
        )

        @pl.when(period == 1)
        def _():
            total[...] += transposed_product(
                moved[span(upper * wide, wide), :], pair[span(lower * states, states), :]
            )

    row = lax.broadcasted_iota(jnp.int32, (level, level), 0)
    column = lax.broadcasted_iota(jnp.int32, (level, level), 1)
    upper_part = row <= column

    def folded(value):
        return [value[:rows, :], value[rows:, :]]

    def diagonal(point, which):
        block(which, which)
        blocks[point, which, span(which * wide, wide), :] = total[...].astype(jnp.bfloat16)
        real = total[:level, level : 2 * level]
        imag = total[:level, 3 * level :]
        cross[which, point] = jnp.concatenate(folded(real) + folded(imag), axis=1).astype(
            jnp.bfloat16
        )
        for bit in range(2):
            at = slice(bit * level, (bit + 1) * level)
            packed = jnp.where(
                upper_part,
                total[at, bit * level : (bit + 1) * level],
                total[at, (2 + bit) * level : (3 + bit) * level],
            )
            kept = jnp.concatenate(folded(packed), axis=1).astype(jnp.bfloat16)
            for member in range(points):

                @pl.when(point == member)
                def _():
                    diag[which, bit, :, member * wide : (member + 1) * wide] = kept

    def crossing(point, which):
        block(which, 1 - which)
        blocks[point, 1 - which, span(which * wide, wide), :] = total[...].astype(jnp.bfloat16)

    @pl.loop(0, points)
    def _(point):
        @pl.when(point == 0)
        def _():
            small[0].wait()

        fill_stack(point)

        @pl.when(period == 1)
        def _():
            @pl.when(point == 0)
            def _():
                small[1].wait()

            fill_pair(point)

            @pl.when(point == 0)
            def _():
                pl.semaphore_wait(barrier, groups)

            hand(point).wait_recv()
            fill_moved(point)

        @pl.loop(0, 2)
        def _(step):
            which = jnp.where(step == 0, far, half)
            diagonal(point, which)

            @pl.when((period == 0) & (point == 0) & (step == 0))
            def _():
                pl.semaphore_wait(barrier, groups)

            @pl.when(step == 0)
            def _():
                send_c(point, far, 0, far_near).start()

                @pl.when(point == points - 1)
                def _():
                    send_o().start()
                    send_d(far, 1 - far, 0, far_near).start()

            @pl.when(step == 1)
            def _():
                send_c(point, half, 1, beside).start()
                send_c(point, half, 2, across).start()
                own_c(point).start()

                @pl.when(point == points - 1)
                def _():
                    send_d(half, low, 1, beside).start()
                    send_d(half, 1 - low, 2, across).start()
                    own_d().start()

            crossing(point, which)

            @pl.when(step == 0)
            def _():
                for device in (
                    4 * far + 2 * far + 1 - side,
                    4 * far + 2 * half + 1 - side,
                    4 * far + 2 * far + side,
                    4 * far + 2 * half + side,
                ):
                    send_x(point, device).start()

            @pl.when(step == 1)
            def _():
                for device in (2 * other + 1 - side, across, beside):
                    send_x(point, device).start()
                own_x(point).start()

        @pl.when(period == 0)
        def _():
            hand(point).start()

    @pl.when(period == 0)
    def _():
        small[1].wait()

    def pass_c(point, source, slot):
        side_c(point, source).wait_recv()
        if slot is not None:

            @pl.when(at_entry)
            def _():
                on_c(point, source, slot).start()

        side_c(point, source).start()

    def pass_d(source, slot):
        if slot is not None:

            @pl.when(at_entry)
            def _():
                wait_o(slot, source)
                on_o(slot, source).start()

        side_d(source).wait_recv()
        side_d(source).start()

    passing = ((far_near, 0), (across, None), (far_end, 1))
    for point in range(points):
        for source, slot in passing:
            pass_c(point, source, slot)
    for source, slot in passing:
        pass_d(source, slot)

    small[2].wait()
    small[3].wait()
    long = count * SUB
    source_of = index[...]
    value_of = weight[...]
    target = lax.broadcasted_iota(jnp.int32, (count, count), 1)
    matrix = jnp.zeros((count, count), jnp.float32)
    for tap in range(index.shape[1]):
        matrix = matrix + jnp.where(
            source_of[:, tap : tap + 1] == target, value_of[:, tap : tap + 1], 0.0
        )
    matrix = matrix.astype(jnp.bfloat16)

    def ones(mask):
        return jnp.where(mask, 1.0, 0.0).astype(jnp.bfloat16)

    def iota(shape, axis):
        return lax.broadcasted_iota(jnp.int32, shape, axis)

    tall = ones(iota((long, count), 0) // SUB == iota((long, count), 1))
    grown = product(tall, matrix).astype(jnp.bfloat16)
    spread[...] = jnp.where(
        iota((long, long), 0) % SUB == iota((long, long), 1) % SUB,
        transposed_product(grown, tall),
        0.0,
    ).astype(jnp.bfloat16)
    short = groups * SUB
    for member in range(points):
        picked = ones(
            (iota((short, count), 0) // SUB) * points + member == iota((short, count), 1)
        )
        spread_d[member] = jnp.where(
            iota((long, short), 0) % SUB == iota((long, short), 1) % SUB,
            transposed_product(grown, picked),
            0.0,
        ).astype(jnp.bfloat16)

    own_d().wait()
    for point in range(points):
        own_c(point).wait()
    for stage in range(groups // 2):
        source = 2 * stage + 1 - side
        for point in range(points):
            side_c(point, source).wait_recv()
        side_d(source).wait_recv()

    @pl.loop(0, rows // SUB)
    def _(at):
        here = span(at * SUB, SUB)
        after = span(rows + at * SUB, SUB)
        value = product(spread[...], got_c[:, :, here, :].reshape(long, states))
        res_c[:, here, :] = value.astype(jnp.bfloat16).reshape(count, SUB, states)
        value = pltpu.roll(value, states - level, 1)
        res_c[:, after, :] = value.astype(jnp.bfloat16).reshape(count, SUB, states)
        taken = got_d[:, here, :].reshape(short, states)
        value = (
            product(spread_d[0], taken)[:, :wide] + product(spread_d[1], taken)[:, wide:]
        )
        first = value[:, :level].astype(jnp.bfloat16)
        second = value[:, level:].astype(jnp.bfloat16)
        res_d[:, here, :] = first.reshape(count, SUB, level)
        res_d[:, after, :] = second.reshape(count, SUB, level)

    row_at = iota((rows, level), 0) + side * rows
    column_at = iota((rows, level), 1)
    pick = ones(row_at == column_at)
    outer = low == 0

    @pl.loop(0, count)
    def _(t):
        mine = span(side * rows, rows)
        straight = res_d[t, mine, :].astype(jnp.float32)
        turned = transposed_product(pick, res_d[t])
        own_real = jnp.where(column_at >= row_at, straight, turned)
        own_imag = jnp.where(
            column_at < row_at, straight, jnp.where(column_at > row_at, -turned, 0.0)
        )
        taken = res_c[t, mine, :].astype(jnp.float32)
        real = transposed_product(pick, res_c[t, :, :level])
        imag = transposed_product(pick, res_c[t, :, 2 * level : 3 * level])
        next_real = jnp.where(outer, taken[:, :level], real)
        next_imag = jnp.where(outer, taken[:, 2 * level : 3 * level], -imag)
        inner[t] = jnp.concatenate(
            [
                jnp.where(outer, own_real, next_real),
                jnp.where(outer, next_real, own_real),
                jnp.where(outer, own_imag, next_imag),
                jnp.where(outer, next_imag, own_imag),
            ],
            axis=1,
        ).astype(jnp.bfloat16)

    for point in range(points):
        own_x(point).wait()
        for step in range(1, groups):
            wait_x(point, (me + step) % groups)

    def store(at):
        here = span(at * SUB, SUB)
        return pltpu.make_async_copy(
            result.at[:, :, here, :], out.at[0, :, :, here, :], out_sem.at[at]
        )

    @pl.loop(0, rows // SUB)
    def _(at):
        here = span(at * SUB, SUB)
        value = product(spread[...], got_x[:, :, here, :].reshape(long, states))
        near = inner[:, here, :].reshape(long, states).astype(jnp.float32)
        first = jnp.where(half == 0, near, value)
        second = jnp.where(half == 0, value, near)
        real = jnp.concatenate([first[:, :wide], second[:, :wide]], axis=1)
        imag = jnp.concatenate([first[:, wide:], second[:, wide:]], axis=1)
        result[:, 0, here, :] = real.astype(jnp.bfloat16).reshape(count, SUB, states)
        result[:, 1, here, :] = imag.astype(jnp.bfloat16).reshape(count, SUB, states)
        store(at).start()

    for point in range(points):
        for step in range(1, groups):
            send_x(point, (me + step) % groups).wait_send()
        send_c(point, far, 0, far_near).wait_send()
        send_c(point, half, 1, beside).wait_send()
        send_c(point, half, 2, across).wait_send()
        for source, slot in passing:
            side_c(point, source).wait_send()
            if slot is not None:

                @pl.when(at_entry)
                def _():
                    on_c(point, source, slot).wait_send()

    send_o().wait_send()
    send_d(far, 1 - far, 0, far_near).wait_send()
    send_d(half, low, 1, beside).wait_send()
    send_d(half, 1 - low, 2, across).wait_send()
    for source, slot in passing:
        side_d(source).wait_send()
        if slot is not None:

            @pl.when(at_entry)
            def _():
                on_o(slot, source).wait_send()

    @pl.when(period == 0)
    def _():
        for point in range(points):
            hand(point).wait_send()

    for at in range(rows // SUB):
        store(at).wait()


def fused_body(groups, retarded, scatter_root, coupling, source_index, kernel_weight):
    points = retarded.shape[1]
    states = retarded.shape[3]
    rows = states // groups
    count = points * groups
    dma = pltpu.SemaphoreType.DMA
    kept = jnp.bfloat16
    anywhere = pl.BlockSpec(memory_space=pl.ANY)
    return pl.pallas_call(
        fused,
        out_shape=jax.ShapeDtypeStruct((1, count, 2, rows, states), kept),
        in_specs=[anywhere] * 5,
        out_specs=anywhere,
        scratch_shapes=[
            pltpu.VMEM((points, 2, states, states), kept),
            pltpu.VMEM(scatter_root.shape, jnp.float32),
            pltpu.VMEM((states, states), kept),
            pltpu.VMEM(source_index.shape, jnp.int32),
            pltpu.VMEM(kernel_weight.shape, jnp.float32),
            pltpu.VMEM((2 * states, 2 * states), kept),
            pltpu.VMEM((2 * states, 2 * states), kept),
            pltpu.VMEM((states, 2 * states), kept),
            pltpu.VMEM((states // 2, states), jnp.float32),
            pltpu.VMEM((points, 2, states, states), kept),
            pltpu.VMEM((points, 2, states, states), kept),
            pltpu.VMEM((2, points, rows, states), kept),
            pltpu.VMEM((2, 2, rows, states), kept),
            pltpu.VMEM((groups, points, rows, states), kept),
            pltpu.VMEM((groups, points, rows, states), kept),
            pltpu.VMEM((groups, rows, states), kept),
            pltpu.VMEM((2, rows, states), kept),
            pltpu.VMEM((count, 2 * rows, states), kept),
            pltpu.VMEM((count, 2 * rows, states // 4), kept),
            pltpu.VMEM((count, rows, states), kept),
            pltpu.VMEM((count, 2, rows, states), kept),
            pltpu.VMEM((count * SUB, count * SUB), kept),
            pltpu.VMEM((points, count * SUB, groups * SUB), kept),
            dma((points, 2)),
            dma((4,)),
            dma((points,)),
            dma((points,)),
            dma,
            dma((groups, points)),
            dma((groups, points)),
            dma((3, points)),
            dma((groups, points)),
            dma((2, points)),
            dma((groups, points)),
            dma((3,)),
            dma((groups,)),
            dma((groups,)),
            dma,
            dma((2,)),
            dma((2,)),
            dma((points,)),
            dma((points,)),
            dma((rows // SUB,)),
        ],
        compiler_params=pltpu.CompilerParams(
            collective_id=0, has_side_effects=True, vmem_limit_bytes=LIMIT * 1024 * 1024
        ),
    )(retarded, scatter_root, coupling, source_index, kernel_weight)


def solution(mesh):
    groups = mesh.shape["ek"]

    def chosen(retarded, *others):
        states = retarded.shape[3]
        fits = (
            groups == 8
            and retarded.shape[1] == 2
            and mesh.shape["per"] == 2
            and states % (groups * SUB) == 0
        )
        if fits:
            return fused_body(groups, retarded, *others)
        return body(retarded, *others)

    in_specs = (
        P("per", ("grp", "ek"), None, None, None),
        P("per", ("grp", "ek"), None),
        P(),
        P(),
        P(),
    )
    out_specs = P("per", "grp", None, "ek", None)
    return jax.shard_map(chosen, mesh=mesh, in_specs=in_specs, out_specs=out_specs, check_vma=False)
```

```python
import jax
import jax.numpy as jnp
from jax import lax
from jax.experimental import pallas as pl
from jax.experimental.pallas import tpu as pltpu
from jax.sharding import PartitionSpec as P


def shifted(array, axis, by):
    size = lax.axis_size(axis)
    pairs = [(i, i + by) for i in range(size) if 0 <= i + by < size]
    return lax.ppermute(array, axis, pairs)


def product(former, latter):
    return jnp.dot(former, latter, preferred_element_type=jnp.float32)


def transposed_product(former, latter):
    return lax.dot_general(
        former, latter, (((1,), (1,)), ((), ())), preferred_element_type=jnp.float32
    )


def build_kernel(source_index, kernel_weight, total_points):
    targets = jnp.arange(total_points, dtype=jnp.int32)
    matches = (source_index[:, :, None] == targets[None, None, :]).astype(jnp.float32)
    return jnp.sum(kernel_weight[:, :, None] * matches, axis=1).astype(jnp.bfloat16)


def local_parts(real_g, imag_g, amplitude):
    root_real = (real_g * amplitude[None, :]).astype(jnp.bfloat16)
    root_imag = (imag_g * amplitude[None, :]).astype(jnp.bfloat16)
    local_real = transposed_product(root_real, root_real) + transposed_product(root_imag, root_imag)
    skewed = transposed_product(root_imag, root_real)
    return (local_real, skewed - skewed.T)


def coupled_parts(real_g, imag_g, coupling):
    return (
        product(real_g, coupling).astype(jnp.bfloat16),
        product(imag_g, coupling).astype(jnp.bfloat16),
    )


def advance(local_pair, coupled_pair, carried_in):
    coupled_real, coupled_imag = coupled_pair
    prev_real = carried_in[0]
    prev_imag = carried_in[1]
    carried_real = (product(coupled_real, prev_real) - product(coupled_imag, prev_imag)).astype(
        jnp.bfloat16
    )
    carried_imag = (product(coupled_real, prev_imag) + product(coupled_imag, prev_real)).astype(
        jnp.bfloat16
    )
    new_real = (
        local_pair[0]
        + transposed_product(carried_real, coupled_real)
        + transposed_product(carried_imag, coupled_imag)
    )
    new_imag = (
        local_pair[1]
        + transposed_product(carried_imag, coupled_real)
        - transposed_product(carried_real, coupled_imag)
    )
    return jnp.stack([new_real.astype(jnp.bfloat16), new_imag.astype(jnp.bfloat16)])


def body(retarded, scatter_root, coupling, source_index, kernel_weight):
    points_dev = retarded.shape[1]
    states = retarded.shape[3]
    groups = lax.axis_size("ek")
    total_points = points_dev * groups
    row_count = states // groups
    kernel = build_kernel(source_index, kernel_weight, total_points)
    local_terms = []
    coupled_terms = []
    lesser = []
    for member in range(points_dev):
        real_g = retarded[0, member, 0]
        imag_g = retarded[0, member, 1]
        local_pair = local_parts(real_g, imag_g, scatter_root[0, member])
        local_terms.append(local_pair)
        coupled_terms.append(coupled_parts(real_g, imag_g, coupling))
        lesser.append(
            jnp.stack([local_pair[0].astype(jnp.bfloat16), local_pair[1].astype(jnp.bfloat16)])
        )
    carried = shifted(jnp.stack(lesser), "per", 1)
    lesser = [
        advance(local_terms[member], coupled_terms[member], carried[member])
        for member in range(points_dev)
    ]
    stacked = jnp.stack(lesser)[None]
    regrouped = lax.all_to_all(stacked, "ek", split_axis=3, concat_axis=1, tiled=True)
    summed = product(kernel, regrouped.reshape(total_points, -1))
    return summed.astype(jnp.bfloat16).reshape(1, total_points, 2, row_count, states)


SUB = 16
LIMIT = 54
MESH = pl.DeviceIdType.MESH


def fused(
    retarded,
    scatter_ref,
    coupling_ref,
    index_ref,
    weight_ref,
    out,
    green,
    scatter,
    coupling,
    index,
    weight,
    stack,
    pair,
    moved,
    total,
    blocks,
    before,
    cross,
    diag,
    got_x,
    got_c,
    got_d,
    got_o,
    res_c,
    res_d,
    inner,
    spread,
    spread_d,
    load_sem,
    small_sem,
    keep_x,
    keep_c,
    keep_d,
    x_send,
    x_recv,
    c_send,
    c_side,
    c_on,
    c_recv,
    d_send,
    d_side,
    d_recv,
    o_send,
    o_on,
    o_recv,
    hand_sem,
    take_sem,
):
    groups, points = got_x.shape[:2]
    me = lax.axis_index("ek")
    period = lax.axis_index("per")
    states = green.shape[2]
    wide = states // 2
    level = states // 4
    rows = states // groups
    count = points * groups

    half = me // 4
    place = me // 2
    side = me % 2
    low = place % 2
    far = 1 - half
    entry = 1 + half
    other = 4 * half + 1 - place
    beside = 2 * place + 1 - side
    across = 2 * other + side
    far_near = 2 * (2 - half) + side
    far_end = 2 * (3 * far) + side
    at_entry = place == entry
    turned = (place + period) % 2

    def load(point, part):
        return pltpu.make_async_copy(
            retarded.at[0, point, part], green.at[point, part], load_sem.at[point, part]
        )

    small = [
        pltpu.make_async_copy(scatter_ref, scatter, small_sem.at[0]),
        pltpu.make_async_copy(coupling_ref, coupling, small_sem.at[1]),
        pltpu.make_async_copy(index_ref, index, small_sem.at[2]),
        pltpu.make_async_copy(weight_ref, weight, small_sem.at[3]),
    ]
    small[0].start()
    for part in range(2):
        load(0, part).start()
    small[1].start()
    for part in range(2):
        load(1, part).start()
    small[2].start()
    small[3].start()

    barrier = pltpu.get_barrier_semaphore()
    for step in range(1, groups):
        pl.semaphore_signal(
            barrier, inc=1, device_id={"ek": (me + step) % groups}, device_id_type=MESH
        )
    pl.semaphore_signal(barrier, inc=1, device_id={"per": 1 - period}, device_id_type=MESH)

    def span(start, size):
        return pl.ds(pl.multiple_of(start, SUB), size)

    def lanes(which):
        return pl.ds(pl.multiple_of(which * states, states), states)

    def remote(source, target, sent, landed, device):
        return pltpu.make_async_remote_copy(
            src_ref=source,
            dst_ref=target,
            send_sem=sent,
            recv_sem=landed,
            device_id={"ek": device},
            device_id_type=MESH,
        )

    def send_x(point, device):
        return remote(
            blocks.at[point, span(device * rows, rows), lanes(1 - device // 4)],
            got_x.at[me, point],
            x_send.at[device, point],
            x_recv.at[me, point],
            device,
        )

    def wait_x(point, device):
        remote(
            got_x.at[device, point],
            got_x.at[device, point],
            x_send.at[device, point],
            x_recv.at[device, point],
            device,
        ).wait_recv()

    def send_c(point, which, slot, device):
        return remote(
            cross.at[which, point],
            got_c.at[me, point],
            c_send.at[slot, point],
            c_recv.at[me, point],
            device,
        )

    def side_c(point, source):
        here = got_c.at[source, point]
        return remote(here, here, c_side.at[source, point], c_recv.at[source, point], beside)

    def on_c(point, source, slot):
        here = got_c.at[source, point]
        return remote(here, here, c_on.at[slot, point], c_recv.at[source, point], across)

    def send_d(which, bit, slot, device):
        return remote(
            diag.at[which, bit], got_d.at[me], d_send.at[slot], d_recv.at[me], device
        )

    def side_d(source):
        here = got_d.at[source]
        return remote(here, here, d_side.at[source], d_recv.at[source], beside)

    def send_o():
        slot = jnp.where(at_entry, 0, 1)
        return remote(
            diag.at[far, far], got_o.at[slot], o_send, o_recv.at[slot], far_near
        )

    def wait_o(slot, source):
        remote(
            got_o.at[slot], got_o.at[slot], o_on.at[slot], o_recv.at[slot], source
        ).wait_recv()

    def on_o(slot, source):
        return remote(
            got_o.at[slot], got_d.at[source], o_on.at[slot], d_recv.at[source], across
        )

    def hand(point):
        return pltpu.make_async_remote_copy(
            src_ref=blocks.at[point],
            dst_ref=before.at[point],
            send_sem=hand_sem.at[point],
            recv_sem=take_sem.at[point],
            device_id={"per": 1 - period},
            device_id_type=MESH,
        )

    def own_x(point):
        return pltpu.make_async_copy(
            blocks.at[point, span(me * rows, rows), lanes(far)],
            got_x.at[me, point],
            keep_x.at[point],
        )

    def own_c(point):
        return pltpu.make_async_copy(
            cross.at[half, point], got_c.at[me, point], keep_c.at[point]
        )

    def own_d():
        return pltpu.make_async_copy(diag.at[half, low], got_d.at[me], keep_d)

    long = count * SUB
    short = groups * SUB

    def ones(mask):
        return jnp.where(mask, 1.0, 0.0).astype(jnp.bfloat16)

    def iota(shape, axis):
        return lax.broadcasted_iota(jnp.int32, shape, axis)

    def fill_spread():
        small[2].wait()
        small[3].wait()
        source_of = index[...]
        value_of = weight[...]
        target = lax.broadcasted_iota(jnp.int32, (count, count), 1)
        matrix = jnp.zeros((count, count), jnp.float32)
        for tap in range(index.shape[1]):
            matrix = matrix + jnp.where(
                source_of[:, tap : tap + 1] == target, value_of[:, tap : tap + 1], 0.0
            )
        matrix = matrix.astype(jnp.bfloat16)

        tall = ones(iota((long, count), 0) // SUB == iota((long, count), 1))
        grown = product(tall, matrix).astype(jnp.bfloat16)
        spread[...] = jnp.where(
            iota((long, long), 0) % SUB == iota((long, long), 1) % SUB,
            transposed_product(grown, tall),
            0.0,
        ).astype(jnp.bfloat16)
        for member in range(points):
            picked = ones(
                (iota((short, count), 0) // SUB) * points + member == iota((short, count), 1)
            )
            spread_d[member] = jnp.where(
                iota((long, short), 0) % SUB == iota((long, short), 1) % SUB,
                transposed_product(grown, picked),
                0.0,
            ).astype(jnp.bfloat16)

    def fill_stack(point):
        for part in range(2):
            load(point, part).wait()
        scale = scatter[0, pl.ds(point, 1), :]
        for band in range(2):
            at = slice(band * wide, (band + 1) * wide)
            real = (green[point, 0, at, :].astype(jnp.float32) * scale).astype(jnp.bfloat16)
            imag = (green[point, 1, at, :].astype(jnp.float32) * scale).astype(jnp.bfloat16)
            top = slice(band * states, band * states + wide)
            low_at = slice(band * states + wide, (band + 1) * states)
            stack[top, :states] = real
            stack[top, states:] = imag
            stack[low_at, :states] = -imag
            stack[low_at, states:] = real

    def fill_pair(point):
        real = product(green[point, 0], coupling[...]).astype(jnp.bfloat16)
        imag = product(green[point, 1], coupling[...]).astype(jnp.bfloat16)
        for band in range(2):
            at = slice(band * wide, (band + 1) * wide)
            top = slice(band * states, band * states + wide)
            low_at = slice(band * states + wide, (band + 1) * states)
            pair[top, :states] = real[at, :]
            pair[top, states:] = imag[at, :]
            pair[low_at, :states] = -imag[at, :]
            pair[low_at, states:] = real[at, :]

    def fill_moved(point):
        @pl.loop(0, 2)
        def _(band):
            at = span(band * wide, wide)
            top = span(band * states, wide)
            straight = product(pair[top, :states], before[point])
            swapped = product(pair[top, states:], before[point])
            for part in range(2):
                left = slice(part * states, part * states + wide)
                right = slice(part * states + wide, (part + 1) * states)
                real = straight[:, left] - swapped[:, right]
                imag = straight[:, right] + swapped[:, left]
                moved[at, part * wide : (part + 1) * wide] = real.astype(jnp.bfloat16)
                moved[at, states + part * wide : states + (part + 1) * wide] = imag.astype(
                    jnp.bfloat16
                )

    def block(point):
        @pl.loop(0, 2)
        def _(band):
            at = span(band * wide, wide)
            total[at, :] = transposed_product(stack[span(band * states, wide), :], stack[...])

            @pl.when(period == 1)
            def _():
                total[at, :] += transposed_product(moved[at, :], pair[...])

            blocks[point, at, :] = total[at, :].astype(jnp.bfloat16)

    upper_part = lax.broadcasted_iota(jnp.int32, (level, level), 0) <= lax.broadcasted_iota(
        jnp.int32, (level, level), 1
    )

    def folded(value):
        return [value[:rows, :], value[rows:, :]]

    def diagonal(point, which):
        value = total[span(which * wide, wide), lanes(which)]
        real = value[:level, level : 2 * level]
        imag = value[:level, 3 * level :]
        cross[which, point] = jnp.concatenate(folded(real) + folded(imag), axis=1).astype(
            jnp.bfloat16
        )
        for bit in range(2):
            at = slice(bit * level, (bit + 1) * level)
            packed = jnp.where(
                upper_part,
                value[at, bit * level : (bit + 1) * level],
                value[at, (2 + bit) * level : (3 + bit) * level],
            )
            kept = jnp.concatenate(folded(packed), axis=1).astype(jnp.bfloat16)
            for member in range(points):

                @pl.when(point == member)
                def _():
                    diag[which, bit, :, member * wide : (member + 1) * wide] = kept

    def send_far(point):
        for turn, at_level in enumerate((far, far, half, half)):
            column = (side + turn + turned) % 2
            send_x(point, 4 * far + 2 * at_level + column).start()

    def send_near(point):
        for device in (2 * other + 1 - side, across, beside):
            send_x(point, device).start()

    @pl.loop(0, points)
    def _(point):
        @pl.when(point == 0)
        def _():
            small[0].wait()

        fill_stack(point)

        @pl.when(period == 1)
        def _():
            @pl.when(point == 0)
            def _():
                small[1].wait()

            fill_pair(point)

            @pl.when(point == 0)
            def _():
                pl.semaphore_wait(barrier, groups)

            @pl.when(point == 0)
            def _():
                fill_spread()

            hand(point).wait_recv()
            fill_moved(point)

        block(point)

        @pl.when((period == 0) & (point == 0))
        def _():
            pl.semaphore_wait(barrier, groups)

        @pl.when(period == 0)
        def _():
            hand(point).start()

        @pl.loop(0, 2)
        def _(step):
            which = jnp.where((step == 0) == at_entry, far, half)
            diagonal(point, which)

            @pl.when((which == far) & at_entry)
            def _():
                send_c(point, far, 0, far_near).start()

                @pl.when(point == points - 1)
                def _():
                    send_o().start()
                    send_d(far, 1 - far, 0, far_near).start()

            @pl.when(which == half)
            def _():
                send_c(point, half, 1, beside).start()
                send_c(point, half, 2, across).start()
                own_c(point).start()

                @pl.when(point == points - 1)
                def _():
                    send_d(half, low, 1, beside).start()
                    send_d(half, 1 - low, 2, across).start()
                    own_d().start()

            @pl.when((which == far) & at_entry & (period == 0))
            def _():
                send_far(point)

            @pl.when(which == half)
            def _():
                own_x(point).start()

            @pl.when((which == half) & (period == 0))
            def _():
                send_near(point)

    @pl.when(~at_entry)
    def _():
        for point in range(points):
            send_c(point, far, 0, far_near).start()
        send_o().start()
        send_d(far, 1 - far, 0, far_near).start()

    @pl.when(~at_entry | (period == 1))
    def _():
        for point in range(points):
            send_far(point)

    @pl.when(period == 1)
    def _():
        for point in range(points):
            send_near(point)

    @pl.when(period == 0)
    def _():
        small[1].wait()
        fill_spread()

    def pass_c(point, source, slot):
        side_c(point, source).wait_recv()
        if slot is not None:

            @pl.when(at_entry)
            def _():
                on_c(point, source, slot).start()

        side_c(point, source).start()

    def pass_d(source, slot):
        if slot is not None:

            @pl.when(at_entry)
            def _():
                wait_o(slot, source)
                on_o(slot, source).start()

        side_d(source).wait_recv()
        side_d(source).start()

    passing = ((far_near, 0), (across, None), (far_end, 1))
    for source, slot in passing:
        for point in range(points):
            pass_c(point, source, slot)
        pass_d(source, slot)

    own_d().wait()
    for point in range(points):
        own_c(point).wait()
    for stage in range(groups // 2):
        source = 2 * stage + 1 - side
        for point in range(points):
            side_c(point, source).wait_recv()
        side_d(source).wait_recv()

    @pl.loop(0, rows // SUB, unroll=True)
    def _(at):
        here = span(at * SUB, SUB)
        after = span(rows + at * SUB, SUB)
        value = product(spread[...], got_c[:, :, here, :].reshape(long, states))
        res_c[:, here, :] = value.astype(jnp.bfloat16).reshape(count, SUB, states)
        value = pltpu.roll(value, states - level, 1)
        res_c[:, after, :] = value.astype(jnp.bfloat16).reshape(count, SUB, states)
        taken = got_d[:, here, :].reshape(short, states)
        value = (
            product(spread_d[0], taken)[:, :wide] + product(spread_d[1], taken)[:, wide:]
        )
        first = value[:, :level].astype(jnp.bfloat16)
        second = value[:, level:].astype(jnp.bfloat16)
        res_d[:, here, :] = first.reshape(count, SUB, level)
        res_d[:, after, :] = second.reshape(count, SUB, level)

    row_at = iota((rows, level), 0) + side * rows
    column_at = iota((rows, level), 1)
    pick = ones(row_at == column_at)
    outer = low == 0

    @pl.loop(0, count, unroll=8)
    def _(t):
        mine = span(side * rows, rows)
        straight = res_d[t, mine, :].astype(jnp.float32)
        mirrored = transposed_product(pick, res_d[t])
        own_real = jnp.where(column_at >= row_at, straight, mirrored)
        own_imag = jnp.where(
            column_at < row_at, straight, jnp.where(column_at > row_at, -mirrored, 0.0)
        )
        taken = res_c[t, mine, :].astype(jnp.float32)
        real = transposed_product(pick, res_c[t, :, :level])
        imag = transposed_product(pick, res_c[t, :, 2 * level : 3 * level])
        next_real = jnp.where(outer, taken[:, :level], real)
        next_imag = jnp.where(outer, taken[:, 2 * level : 3 * level], -imag)
        real = jnp.concatenate(
            [jnp.where(outer, own_real, next_real), jnp.where(outer, next_real, own_real)], axis=1
        ).astype(jnp.bfloat16)
        imag = jnp.concatenate(
            [jnp.where(outer, own_imag, next_imag), jnp.where(outer, next_imag, own_imag)], axis=1
        ).astype(jnp.bfloat16)
        inner[t, 0] = real
        inner[t, 1] = imag

    for which in range(2):

        @pl.when(half == which)
        def _():
            out[0, :, :, :, which * wide : (which + 1) * wide] = inner[...]

    for point in range(points):
        own_x(point).wait()
        for step in range(1, groups):
            wait_x(point, (me + step) % groups)

    @pl.loop(0, rows // SUB, unroll=True)
    def _(at):
        here = span(at * SUB, SUB)
        value = product(spread[...], got_x[:, :, here, :].reshape(long, states))
        real = value[:, :wide].astype(jnp.bfloat16).reshape(count, SUB, wide)
        imag = value[:, wide:].astype(jnp.bfloat16).reshape(count, SUB, wide)
        inner[:, 0, here, :] = real
        inner[:, 1, here, :] = imag

    for which in range(2):

        @pl.when(far == which)
        def _():
            out[0, :, :, :, which * wide : (which + 1) * wide] = inner[...]

    for point in range(points):
        for step in range(1, groups):
            send_x(point, (me + step) % groups).wait_send()
        send_c(point, far, 0, far_near).wait_send()
        send_c(point, half, 1, beside).wait_send()
        send_c(point, half, 2, across).wait_send()
        for source, slot in passing:
            side_c(point, source).wait_send()
            if slot is not None:

                @pl.when(at_entry)
                def _():
                    on_c(point, source, slot).wait_send()

    send_o().wait_send()
    send_d(far, 1 - far, 0, far_near).wait_send()
    send_d(half, low, 1, beside).wait_send()
    send_d(half, 1 - low, 2, across).wait_send()
    for source, slot in passing:
        side_d(source).wait_send()
        if slot is not None:

            @pl.when(at_entry)
            def _():
                on_o(slot, source).wait_send()

    @pl.when(period == 0)
    def _():
        for point in range(points):
            hand(point).wait_send()


def fused_body(groups, retarded, scatter_root, coupling, source_index, kernel_weight):
    points = retarded.shape[1]
    states = retarded.shape[3]
    rows = states // groups
    count = points * groups
    dma = pltpu.SemaphoreType.DMA
    kept = jnp.bfloat16
    far_off = pl.BlockSpec(memory_space=pltpu.HBM)
    return pl.pallas_call(
        fused,
        out_shape=pltpu.VMEM((1, count, 2, rows, states), kept),
        in_specs=[far_off] * 5,
        out_specs=pl.BlockSpec(memory_space=pltpu.VMEM),
        scratch_shapes=[
            pltpu.VMEM((points, 2, states, states), kept),
            pltpu.VMEM(scatter_root.shape, jnp.float32),
            pltpu.VMEM((states, states), kept),
            pltpu.VMEM(source_index.shape, jnp.int32),
            pltpu.VMEM(kernel_weight.shape, jnp.float32),
            pltpu.VMEM((2 * states, 2 * states), kept),
            pltpu.VMEM((2 * states, 2 * states), kept),
            pltpu.VMEM((states, 2 * states), kept),
            pltpu.VMEM((states, 2 * states), jnp.float32),
            pltpu.VMEM((points, states, 2 * states), kept),
            pltpu.VMEM((points, states, 2 * states), kept),
            pltpu.VMEM((2, points, rows, states), kept),
            pltpu.VMEM((2, 2, rows, states), kept),
            pltpu.VMEM((groups, points, rows, states), kept),
            pltpu.VMEM((groups, points, rows, states), kept),
            pltpu.VMEM((groups, rows, states), kept),
            pltpu.VMEM((2, rows, states), kept),
            pltpu.VMEM((count, 2 * rows, states), kept),
            pltpu.VMEM((count, 2 * rows, states // 4), kept),
            pltpu.VMEM((count, 2, rows, states // 2), kept),
            pltpu.VMEM((count * SUB, count * SUB), kept),
            pltpu.VMEM((points, count * SUB, groups * SUB), kept),
            dma((points, 2)),
            dma((4,)),
            dma((points,)),
            dma((points,)),
            dma,
            dma((groups, points)),
            dma((groups, points)),
            dma((3, points)),
            dma((groups, points)),
            dma((2, points)),
            dma((groups, points)),
            dma((3,)),
            dma((groups,)),
            dma((groups,)),
            dma,
            dma((2,)),
            dma((2,)),
            dma((points,)),
            dma((points,)),
        ],
        compiler_params=pltpu.CompilerParams(
            collective_id=0, has_side_effects=True, vmem_limit_bytes=LIMIT * 1024 * 1024
        ),
    )(
        *(
            pltpu.with_memory_space_constraint(array, pltpu.HBM)
            for array in (retarded, scatter_root, coupling, source_index, kernel_weight)
        )
    )


def solution(mesh):
    groups = mesh.shape["ek"]

    def chosen(retarded, *others):
        states = retarded.shape[3]
        fits = (
            groups == 8
            and retarded.shape[1] == 2
            and mesh.shape["per"] == 2
            and states % (groups * SUB) == 0
        )
        if fits:
            return fused_body(groups, retarded, *others)
        return body(retarded, *others)

    in_specs = (
        P("per", ("grp", "ek"), None, None, None),
        P("per", ("grp", "ek"), None),
        P(),
        P(),
        P(),
    )
    out_specs = P("per", "grp", None, "ek", None)
    return jax.shard_map(chosen, mesh=mesh, in_specs=in_specs, out_specs=out_specs, check_vma=False)
```

```python
import jax
import jax.numpy as jnp
from jax import lax
from jax.experimental import pallas as pl
from jax.experimental.pallas import tpu as pltpu
from jax.sharding import PartitionSpec as P


def shifted(array, axis, by):
    size = lax.axis_size(axis)
    pairs = [(i, i + by) for i in range(size) if 0 <= i + by < size]
    return lax.ppermute(array, axis, pairs)


def product(former, latter):
    return jnp.dot(former, latter, preferred_element_type=jnp.float32)


def transposed_product(former, latter):
    return lax.dot_general(
        former, latter, (((1,), (1,)), ((), ())), preferred_element_type=jnp.float32
    )


def build_kernel(source_index, kernel_weight, total_points):
    targets = jnp.arange(total_points, dtype=jnp.int32)
    matches = (source_index[:, :, None] == targets[None, None, :]).astype(jnp.float32)
    return jnp.sum(kernel_weight[:, :, None] * matches, axis=1).astype(jnp.bfloat16)


def local_parts(real_g, imag_g, amplitude):
    root_real = (real_g * amplitude[None, :]).astype(jnp.bfloat16)
    root_imag = (imag_g * amplitude[None, :]).astype(jnp.bfloat16)
    local_real = transposed_product(root_real, root_real) + transposed_product(root_imag, root_imag)
    skewed = transposed_product(root_imag, root_real)
    return (local_real, skewed - skewed.T)


def coupled_parts(real_g, imag_g, coupling):
    return (
        product(real_g, coupling).astype(jnp.bfloat16),
        product(imag_g, coupling).astype(jnp.bfloat16),
    )


def advance(local_pair, coupled_pair, carried_in):
    coupled_real, coupled_imag = coupled_pair
    prev_real = carried_in[0]
    prev_imag = carried_in[1]
    carried_real = (product(coupled_real, prev_real) - product(coupled_imag, prev_imag)).astype(
        jnp.bfloat16
    )
    carried_imag = (product(coupled_real, prev_imag) + product(coupled_imag, prev_real)).astype(
        jnp.bfloat16
    )
    new_real = (
        local_pair[0]
        + transposed_product(carried_real, coupled_real)
        + transposed_product(carried_imag, coupled_imag)
    )
    new_imag = (
        local_pair[1]
        + transposed_product(carried_imag, coupled_real)
        - transposed_product(carried_real, coupled_imag)
    )
    return jnp.stack([new_real.astype(jnp.bfloat16), new_imag.astype(jnp.bfloat16)])


def body(retarded, scatter_root, coupling, source_index, kernel_weight):
    points_dev = retarded.shape[1]
    states = retarded.shape[3]
    groups = lax.axis_size("ek")
    total_points = points_dev * groups
    row_count = states // groups
    kernel = build_kernel(source_index, kernel_weight, total_points)
    local_terms = []
    coupled_terms = []
    lesser = []
    for member in range(points_dev):
        real_g = retarded[0, member, 0]
        imag_g = retarded[0, member, 1]
        local_pair = local_parts(real_g, imag_g, scatter_root[0, member])
        local_terms.append(local_pair)
        coupled_terms.append(coupled_parts(real_g, imag_g, coupling))
        lesser.append(
            jnp.stack([local_pair[0].astype(jnp.bfloat16), local_pair[1].astype(jnp.bfloat16)])
        )
    carried = shifted(jnp.stack(lesser), "per", 1)
    lesser = [
        advance(local_terms[member], coupled_terms[member], carried[member])
        for member in range(points_dev)
    ]
    stacked = jnp.stack(lesser)[None]
    regrouped = lax.all_to_all(stacked, "ek", split_axis=3, concat_axis=1, tiled=True)
    summed = product(kernel, regrouped.reshape(total_points, -1))
    return summed.astype(jnp.bfloat16).reshape(1, total_points, 2, row_count, states)


SUB = 16
LIMIT = 54
MESH = pl.DeviceIdType.MESH


def fused(
    retarded,
    scatter_ref,
    coupling_ref,
    index_ref,
    weight_ref,
    out,
    green,
    scatter,
    coupling,
    index,
    weight,
    stack,
    pair,
    moved,
    total,
    blocks,
    before,
    cross,
    diag,
    got_x,
    got_c,
    got_d,
    got_o,
    res_c,
    res_d,
    inner,
    spread,
    spread_d,
    load_sem,
    small_sem,
    keep_x,
    keep_c,
    keep_d,
    x_send,
    x_recv,
    c_send,
    c_side,
    c_on,
    c_recv,
    d_send,
    d_side,
    d_recv,
    o_send,
    o_on,
    o_recv,
    hand_sem,
    take_sem,
):
    groups, points = got_x.shape[:2]
    me = lax.axis_index("ek")
    period = lax.axis_index("per")
    states = green.shape[2]
    wide = states // 2
    level = states // 4
    rows = states // groups
    count = points * groups

    half = me // 4
    place = me // 2
    side = me % 2
    low = place % 2
    far = 1 - half
    entry = 1 + half
    other = 4 * half + 1 - place
    beside = 2 * place + 1 - side
    across = 2 * other + side
    far_near = 2 * (2 - half) + side
    far_end = 2 * (3 * far) + side
    at_entry = place == entry
    turned = (place + period) % 2

    def load(point, part):
        return pltpu.make_async_copy(
            retarded.at[0, point, part], green.at[point, part], load_sem.at[point, part]
        )

    small = [
        pltpu.make_async_copy(scatter_ref, scatter, small_sem.at[0]),
        pltpu.make_async_copy(coupling_ref, coupling, small_sem.at[1]),
        pltpu.make_async_copy(index_ref, index, small_sem.at[2]),
        pltpu.make_async_copy(weight_ref, weight, small_sem.at[3]),
    ]
    small[0].start()
    for part in range(2):
        load(0, part).start()
    small[1].start()
    for part in range(2):
        load(1, part).start()
    small[2].start()
    small[3].start()

    barrier = pltpu.get_barrier_semaphore()
    for step in range(1, groups):
        pl.semaphore_signal(
            barrier, inc=1, device_id={"ek": (me + step) % groups}, device_id_type=MESH
        )
    pl.semaphore_signal(barrier, inc=1, device_id={"per": 1 - period}, device_id_type=MESH)

    def span(start, size):
        return pl.ds(pl.multiple_of(start, SUB), size)

    def lanes(which):
        return pl.ds(pl.multiple_of(which * states, states), states)

    def remote(source, target, sent, landed, device):
        return pltpu.make_async_remote_copy(
            src_ref=source,
            dst_ref=target,
            send_sem=sent,
            recv_sem=landed,
            device_id={"ek": device},
            device_id_type=MESH,
        )

    def send_x(point, device):
        return remote(
            blocks.at[point, span(device * rows, rows), lanes(1 - device // 4)],
            got_x.at[me, point],
            x_send.at[device, point],
            x_recv.at[me, point],
            device,
        )

    def wait_x(point, device):
        remote(
            got_x.at[device, point],
            got_x.at[device, point],
            x_send.at[device, point],
            x_recv.at[device, point],
            device,
        ).wait_recv()

    def send_c(point, which, slot, device):
        return remote(
            cross.at[which, point],
            got_c.at[me, point],
            c_send.at[slot, point],
            c_recv.at[me, point],
            device,
        )

    def side_c(point, source):
        here = got_c.at[source, point]
        return remote(here, here, c_side.at[source, point], c_recv.at[source, point], beside)

    def on_c(point, source, slot):
        here = got_c.at[source, point]
        return remote(here, here, c_on.at[slot, point], c_recv.at[source, point], across)

    def send_d(which, bit, slot, device):
        return remote(
            diag.at[which, bit], got_d.at[me], d_send.at[slot], d_recv.at[me], device
        )

    def side_d(source):
        here = got_d.at[source]
        return remote(here, here, d_side.at[source], d_recv.at[source], beside)

    def send_o():
        slot = jnp.where(at_entry, 0, 1)
        return remote(
            diag.at[far, far], got_o.at[slot], o_send, o_recv.at[slot], far_near
        )

    def wait_o(slot, source):
        remote(
            got_o.at[slot], got_o.at[slot], o_on.at[slot], o_recv.at[slot], source
        ).wait_recv()

    def on_o(slot, source):
        return remote(
            got_o.at[slot], got_d.at[source], o_on.at[slot], d_recv.at[source], across
        )

    def hand(point):
        return pltpu.make_async_remote_copy(
            src_ref=blocks.at[point],
            dst_ref=before.at[point],
            send_sem=hand_sem.at[point],
            recv_sem=take_sem.at[point],
            device_id={"per": 1 - period},
            device_id_type=MESH,
        )

    def own_x(point):
        return pltpu.make_async_copy(
            blocks.at[point, span(me * rows, rows), lanes(far)],
            got_x.at[me, point],
            keep_x.at[point],
        )

    def own_c(point):
        return pltpu.make_async_copy(
            cross.at[half, point], got_c.at[me, point], keep_c.at[point]
        )

    def own_d():
        return pltpu.make_async_copy(diag.at[half, low], got_d.at[me], keep_d)

    long = count * SUB
    short = groups * SUB

    def ones(mask):
        return jnp.where(mask, 1.0, 0.0).astype(jnp.bfloat16)

    def iota(shape, axis):
        return lax.broadcasted_iota(jnp.int32, shape, axis)

    def fill_spread():
        small[2].wait()
        small[3].wait()
        source_of = index[...]
        value_of = weight[...]
        target = lax.broadcasted_iota(jnp.int32, (count, count), 1)
        matrix = jnp.zeros((count, count), jnp.float32)
        for tap in range(index.shape[1]):
            matrix = matrix + jnp.where(
                source_of[:, tap : tap + 1] == target, value_of[:, tap : tap + 1], 0.0
            )
        matrix = matrix.astype(jnp.bfloat16)

        tall = ones(iota((long, count), 0) // SUB == iota((long, count), 1))
        grown = product(tall, matrix).astype(jnp.bfloat16)
        spread[...] = jnp.where(
            iota((long, long), 0) % SUB == iota((long, long), 1) % SUB,
            transposed_product(grown, tall),
            0.0,
        ).astype(jnp.bfloat16)
        for member in range(points):
            picked = ones(
                (iota((short, count), 0) // SUB) * points + member == iota((short, count), 1)
            )
            spread_d[member] = jnp.where(
                iota((long, short), 0) % SUB == iota((long, short), 1) % SUB,
                transposed_product(grown, picked),
                0.0,
            ).astype(jnp.bfloat16)

    def fill_stack(point):
        for part in range(2):
            load(point, part).wait()
        scale = scatter[0, pl.ds(point, 1), :]
        for band in range(2):
            at = slice(band * wide, (band + 1) * wide)
            real = (green[point, 0, at, :].astype(jnp.float32) * scale).astype(jnp.bfloat16)
            imag = (green[point, 1, at, :].astype(jnp.float32) * scale).astype(jnp.bfloat16)
            top = slice(band * states, band * states + wide)
            low_at = slice(band * states + wide, (band + 1) * states)
            stack[top, :states] = real
            stack[top, states:] = imag
            stack[low_at, :states] = -imag
            stack[low_at, states:] = real

    def fill_pair(point):
        real = product(green[point, 0], coupling[...]).astype(jnp.bfloat16)
        imag = product(green[point, 1], coupling[...]).astype(jnp.bfloat16)
        for band in range(2):
            at = slice(band * wide, (band + 1) * wide)
            top = slice(band * states, band * states + wide)
            low_at = slice(band * states + wide, (band + 1) * states)
            pair[top, :states] = real[at, :]
            pair[top, states:] = imag[at, :]
            pair[low_at, :states] = -imag[at, :]
            pair[low_at, states:] = real[at, :]

    def fill_moved(point):
        @pl.loop(0, 2)
        def _(band):
            at = span(band * wide, wide)
            top = span(band * states, wide)
            straight = product(pair[top, :states], before[point])
            swapped = product(pair[top, states:], before[point])
            for part in range(2):
                left = slice(part * states, part * states + wide)
                right = slice(part * states + wide, (part + 1) * states)
                real = straight[:, left] - swapped[:, right]
                imag = straight[:, right] + swapped[:, left]
                moved[at, part * wide : (part + 1) * wide] = real.astype(jnp.bfloat16)
                moved[at, states + part * wide : states + (part + 1) * wide] = imag.astype(
                    jnp.bfloat16
                )

    def block(point):
        @pl.loop(0, 2)
        def _(band):
            at = span(band * wide, wide)
            total[at, :] = transposed_product(stack[span(band * states, wide), :], stack[...])

            @pl.when(period == 1)
            def _():
                total[at, :] += transposed_product(moved[at, :], pair[...])

            blocks[point, at, :] = total[at, :].astype(jnp.bfloat16)

    upper_part = lax.broadcasted_iota(jnp.int32, (level, level), 0) <= lax.broadcasted_iota(
        jnp.int32, (level, level), 1
    )

    def folded(value):
        return [value[:rows, :], value[rows:, :]]

    def diagonal(point, which):
        value = total[span(which * wide, wide), lanes(which)]
        real = value[:level, level : 2 * level]
        imag = value[:level, 3 * level :]
        cross[which, point] = jnp.concatenate(folded(real) + folded(imag), axis=1).astype(
            jnp.bfloat16
        )
        for bit in range(2):
            at = slice(bit * level, (bit + 1) * level)
            packed = jnp.where(
                upper_part,
                value[at, bit * level : (bit + 1) * level],
                value[at, (2 + bit) * level : (3 + bit) * level],
            )
            kept = jnp.concatenate(folded(packed), axis=1).astype(jnp.bfloat16)
            for member in range(points):

                @pl.when(point == member)
                def _():
                    diag[which, bit, :, member * wide : (member + 1) * wide] = kept

    def send_far(point):
        for turn, at_level in enumerate((far, far, half, half)):
            column = (side + turn + turned) % 2
            send_x(point, 4 * far + 2 * at_level + column).start()

    def send_near(point):
        for device in (2 * other + 1 - side, across, beside):
            send_x(point, device).start()

    @pl.loop(0, points)
    def _(point):
        @pl.when(point == 0)
        def _():
            small[0].wait()

        fill_stack(point)

        @pl.when(period == 1)
        def _():
            @pl.when(point == 0)
            def _():
                small[1].wait()

            fill_pair(point)

            @pl.when(point == 0)
            def _():
                pl.semaphore_wait(barrier, groups)

            @pl.when(point == 0)
            def _():
                fill_spread()

            hand(point).wait_recv()
            fill_moved(point)

        block(point)

        @pl.when((period == 0) & (point == 0))
        def _():
            pl.semaphore_wait(barrier, groups)

        @pl.when(period == 0)
        def _():
            hand(point).start()

        @pl.loop(0, 2)
        def _(step):
            which = jnp.where((step == 0) == at_entry, far, half)
            diagonal(point, which)

            @pl.when((which == far) & at_entry)
            def _():
                send_c(point, far, 0, far_near).start()

                @pl.when(point == points - 1)
                def _():
                    send_o().start()
                    send_d(far, 1 - far, 0, far_near).start()

            @pl.when(which == half)
            def _():
                send_c(point, half, 1, beside).start()
                send_c(point, half, 2, across).start()
                own_c(point).start()

                @pl.when(point == points - 1)
                def _():
                    send_d(half, low, 1, beside).start()
                    send_d(half, 1 - low, 2, across).start()
                    own_d().start()

            @pl.when((which == far) & at_entry & (period == 0))
            def _():
                send_far(point)

            @pl.when(which == half)
            def _():
                own_x(point).start()

            @pl.when((which == half) & (period == 1))
            def _():
                send_near(point)

    @pl.when(~at_entry)
    def _():
        for point in range(points):
            send_c(point, far, 0, far_near).start()
        send_o().start()
        send_d(far, 1 - far, 0, far_near).start()

    @pl.when(~at_entry | (period == 1))
    def _():
        for point in range(points):
            send_far(point)

    @pl.when(period == 0)
    def _():
        small[1].wait()
        fill_spread()

    def pass_c(point, source, slot):
        side_c(point, source).wait_recv()
        if slot is not None:

            @pl.when(at_entry)
            def _():
                on_c(point, source, slot).start()

        side_c(point, source).start()

    def pass_d(source, slot):
        if slot is not None:

            @pl.when(at_entry)
            def _():
                wait_o(slot, source)
                on_o(slot, source).start()

        side_d(source).wait_recv()
        side_d(source).start()

    passing = ((far_near, 0), (across, None), (far_end, 1))
    for source, slot in passing:
        for point in range(points):
            pass_c(point, source, slot)
        pass_d(source, slot)

    @pl.when(period == 0)
    def _():
        for point in range(points):
            send_near(point)

    for point in range(points):
        own_x(point).wait()
        for step in range(1, groups):
            wait_x(point, (me + step) % groups)

    @pl.loop(0, rows // SUB, unroll=True)
    def _(at):
        here = span(at * SUB, SUB)
        value = product(spread[...], got_x[:, :, here, :].reshape(long, states))
        real = value[:, :wide].astype(jnp.bfloat16).reshape(count, SUB, wide)
        imag = value[:, wide:].astype(jnp.bfloat16).reshape(count, SUB, wide)
        inner[:, 0, here, :] = real
        inner[:, 1, here, :] = imag

    for which in range(2):

        @pl.when(far == which)
        def _():
            out[0, :, :, :, which * wide : (which + 1) * wide] = inner[...]

    own_d().wait()
    for point in range(points):
        own_c(point).wait()
    for stage in range(groups // 2):
        source = 2 * stage + 1 - side
        for point in range(points):
            side_c(point, source).wait_recv()
        side_d(source).wait_recv()

    @pl.loop(0, rows // SUB, unroll=True)
    def _(at):
        here = span(at * SUB, SUB)
        after = span(rows + at * SUB, SUB)
        value = product(spread[...], got_c[:, :, here, :].reshape(long, states))
        res_c[:, here, :] = value.astype(jnp.bfloat16).reshape(count, SUB, states)
        value = pltpu.roll(value, states - level, 1)
        res_c[:, after, :] = value.astype(jnp.bfloat16).reshape(count, SUB, states)
        taken = got_d[:, here, :].reshape(short, states)
        value = (
            product(spread_d[0], taken)[:, :wide] + product(spread_d[1], taken)[:, wide:]
        )
        first = value[:, :level].astype(jnp.bfloat16)
        second = value[:, level:].astype(jnp.bfloat16)
        res_d[:, here, :] = first.reshape(count, SUB, level)
        res_d[:, after, :] = second.reshape(count, SUB, level)

    row_at = iota((rows, level), 0) + side * rows
    column_at = iota((rows, level), 1)
    pick = ones(row_at == column_at)
    outer = low == 0

    @pl.loop(0, count, unroll=8)
    def _(t):
        mine = span(side * rows, rows)
        straight = res_d[t, mine, :].astype(jnp.float32)
        mirrored = transposed_product(pick, res_d[t])
        own_real = jnp.where(column_at >= row_at, straight, mirrored)
        own_imag = jnp.where(
            column_at < row_at, straight, jnp.where(column_at > row_at, -mirrored, 0.0)
        )
        taken = res_c[t, mine, :].astype(jnp.float32)
        real = transposed_product(pick, res_c[t, :, :level])
        imag = transposed_product(pick, res_c[t, :, 2 * level : 3 * level])
        next_real = jnp.where(outer, taken[:, :level], real)
        next_imag = jnp.where(outer, taken[:, 2 * level : 3 * level], -imag)
        real = jnp.concatenate(
            [jnp.where(outer, own_real, next_real), jnp.where(outer, next_real, own_real)], axis=1
        ).astype(jnp.bfloat16)
        imag = jnp.concatenate(
            [jnp.where(outer, own_imag, next_imag), jnp.where(outer, next_imag, own_imag)], axis=1
        ).astype(jnp.bfloat16)
        inner[t, 0] = real
        inner[t, 1] = imag

    for which in range(2):

        @pl.when(half == which)
        def _():
            out[0, :, :, :, which * wide : (which + 1) * wide] = inner[...]

    for point in range(points):
        for step in range(1, groups):
            send_x(point, (me + step) % groups).wait_send()
        send_c(point, far, 0, far_near).wait_send()
        send_c(point, half, 1, beside).wait_send()
        send_c(point, half, 2, across).wait_send()
        for source, slot in passing:
            side_c(point, source).wait_send()
            if slot is not None:

                @pl.when(at_entry)
                def _():
                    on_c(point, source, slot).wait_send()

    send_o().wait_send()
    send_d(far, 1 - far, 0, far_near).wait_send()
    send_d(half, low, 1, beside).wait_send()
    send_d(half, 1 - low, 2, across).wait_send()
    for source, slot in passing:
        side_d(source).wait_send()
        if slot is not None:

            @pl.when(at_entry)
            def _():
                on_o(slot, source).wait_send()

    @pl.when(period == 0)
    def _():
        for point in range(points):
            hand(point).wait_send()


def fused_body(groups, retarded, scatter_root, coupling, source_index, kernel_weight):
    points = retarded.shape[1]
    states = retarded.shape[3]
    rows = states // groups
    count = points * groups
    dma = pltpu.SemaphoreType.DMA
    kept = jnp.bfloat16
    far_off = pl.BlockSpec(memory_space=pltpu.HBM)
    return pl.pallas_call(
        fused,
        out_shape=pltpu.VMEM((1, count, 2, rows, states), kept),
        in_specs=[far_off] * 5,
        out_specs=pl.BlockSpec(memory_space=pltpu.VMEM),
        scratch_shapes=[
            pltpu.VMEM((points, 2, states, states), kept),
            pltpu.VMEM(scatter_root.shape, jnp.float32),
            pltpu.VMEM((states, states), kept),
            pltpu.VMEM(source_index.shape, jnp.int32),
            pltpu.VMEM(kernel_weight.shape, jnp.float32),
            pltpu.VMEM((2 * states, 2 * states), kept),
            pltpu.VMEM((2 * states, 2 * states), kept),
            pltpu.VMEM((states, 2 * states), kept),
            pltpu.VMEM((states, 2 * states), jnp.float32),
            pltpu.VMEM((points, states, 2 * states), kept),
            pltpu.VMEM((points, states, 2 * states), kept),
            pltpu.VMEM((2, points, rows, states), kept),
            pltpu.VMEM((2, 2, rows, states), kept),
            pltpu.VMEM((groups, points, rows, states), kept),
            pltpu.VMEM((groups, points, rows, states), kept),
            pltpu.VMEM((groups, rows, states), kept),
            pltpu.VMEM((2, rows, states), kept),
            pltpu.VMEM((count, 2 * rows, states), kept),
            pltpu.VMEM((count, 2 * rows, states // 4), kept),
            pltpu.VMEM((count, 2, rows, states // 2), kept),
            pltpu.VMEM((count * SUB, count * SUB), kept),
            pltpu.VMEM((points, count * SUB, groups * SUB), kept),
            dma((points, 2)),
            dma((4,)),
            dma((points,)),
            dma((points,)),
            dma,
            dma((groups, points)),
            dma((groups, points)),
            dma((3, points)),
            dma((groups, points)),
            dma((2, points)),
            dma((groups, points)),
            dma((3,)),
            dma((groups,)),
            dma((groups,)),
            dma,
            dma((2,)),
            dma((2,)),
            dma((points,)),
            dma((points,)),
        ],
        compiler_params=pltpu.CompilerParams(
            collective_id=0, has_side_effects=True, vmem_limit_bytes=LIMIT * 1024 * 1024
        ),
    )(
        *(
            pltpu.with_memory_space_constraint(array, pltpu.HBM)
            for array in (retarded, scatter_root, coupling, source_index, kernel_weight)
        )
    )


def solution(mesh):
    groups = mesh.shape["ek"]

    def chosen(retarded, *others):
        states = retarded.shape[3]
        fits = (
            groups == 8
            and retarded.shape[1] == 2
            and mesh.shape["per"] == 2
            and states % (groups * SUB) == 0
        )
        if fits:
            return fused_body(groups, retarded, *others)
        return body(retarded, *others)

    in_specs = (
        P("per", ("grp", "ek"), None, None, None),
        P("per", ("grp", "ek"), None),
        P(),
        P(),
        P(),
    )
    out_specs = P("per", "grp", None, "ek", None)
    return jax.shard_map(chosen, mesh=mesh, in_specs=in_specs, out_specs=out_specs, check_vma=False)
```
